128 devices in a mesh: cam: 4 (over y_hi, core), strip: 32 (over x, z, y_lo).
Axes of the slice: x: 4, y: 4 (y_hi: 2, y_lo: 2; y = y_hi * 2 + y_lo), z: 4, core: 2. Of those that a mesh axis runs over, the one named last changes fastest.
Arguments:
- feats: bfloat16 [4, 96, 512, 256], P('cam', 'strip'), may hold values from -6 to 6
- cotangent: bfloat16 [4, 96, 512, 256], P('cam', 'strip'), may hold values from -6 to 6
- conv_w: bfloat16 [9, 8, 32, 32], replicated, may hold values from -0.375 to 0.375
- conv_b: float32 [256], replicated, may hold values from -3 to 3
- w_query: bfloat16 [256, 256], replicated
- w_key: bfloat16 [256, 256], replicated
- w_value: bfloat16 [256, 256], replicated, may hold values from -0.375 to 0.375
- w_out: bfloat16 [256, 256], replicated, may hold values from -0.375 to 0.375
- time_table: bfloat16 [16, 256], replicated, may hold values from -6 to 6
- frame_index: int32 [4], replicated, may hold values from 0 to 15
- block_start: int32 [4, 32, 4, 3], replicated, may hold values from 0 to 10, as said below
- block_count: int32 [4, 32, 4, 3], replicated, may hold values from 0 to 2, as said below
Outputs:
- grad_feats: bfloat16 [4, 96, 512, 256], P('cam', 'strip')
- grad_conv_w: float32 [9, 8, 32, 32], replicated
- grad_conv_b: float32 [256], replicated
The draws below stay inside these ranges and needn't reach their ends.
Inputs may be any that keep to these rules, and one draw needn't show every extreme that they name: `block_start`: start + 2 never passes 12. `block_count`: entries that name the sending view itself, or a target strip before the first or after the last, are 0; all others are 1 to 2. In every draw one strip of one view receives 2 blocks from each of the three strips around it in every other view.
All inputs are finite; a program needn't handle non-finite values.
Results may differ from the reference program's by a relative error of at most 0.022.
The reference program's roundings to bfloat16 on the way (of `slope_b`, `probs_b`, `score_grad` and `query_grad`) count: a program that leaves them out, or rounds other values in their place, can miss the bound.
Values may be sent and summed in bfloat16 or wider, within the bound.
No kernel may reach another device: no remote copies, remote signals or barrier semaphores. Data moves between devices by JAX's collectives and lax.ppermute only.
A program may use at most 192 MiB of HBM per device.

```python
import math
import jax
import jax.numpy as jnp
from jax import lax

C = 256
GROUPS = 8
CG = 32
HEAD_DIM = 64
ATT = 256
BLK = 128
MOSTB = 2
RS = 3
COLS = 512
FRAMES = 16
CAMS = 4
STRIPS = 32
ROWS = 96
NBLK = 12


def spiked_matrix(key, salt):
    base = jax.random.normal(jax.random.fold_in(key, salt), (C, ATT), jnp.float32) * C ** (-0.5)
    return base.astype(jnp.bfloat16)


def draw_w_query(key, part):
    return spiked_matrix(key, 31)


def draw_w_key(key, part):
    return spiked_matrix(key, 41)


def draw_block_start(key, part):
    shape = (CAMS, STRIPS, CAMS, 3)
    return jax.random.randint(jax.random.fold_in(key, 21), shape, 0, NBLK - MOSTB + 1).astype(jnp.int32)


def draw_block_count(key, part):
    shape = (CAMS, STRIPS, CAMS, 3)
    counts = jax.random.randint(jax.random.fold_in(key, 11), shape, 1, MOSTB + 1)
    source = jnp.arange(CAMS)[:, None, None, None]
    strip = jnp.arange(STRIPS)[None, :, None, None]
    target = jnp.arange(CAMS)[None, None, :, None]
    offset = jnp.arange(3)[None, None, None, :]
    lands = strip + offset - 1
    chosen_view = jax.random.randint(jax.random.fold_in(key, 12), (), 0, CAMS)
    chosen_strip = jax.random.randint(jax.random.fold_in(key, 13), (), 1, STRIPS - 1)
    full = (target == chosen_view) & (lands == chosen_strip)
    counts = jnp.where(full, MOSTB, counts)
    keep = (source != target) & (lands >= 0) & (lands < STRIPS)
    return jnp.where(keep, counts, 0).astype(jnp.int32)


def with_ends(values, stream_key, smallest, largest):
    spot = [jax.random.randint(jax.random.fold_in(stream_key, axis), (), 0, length) for axis, length in enumerate(values.shape)]
    longest = values.shape.index(max(values.shape))
    beside = spot[:longest] + [(spot[longest] + 1) % values.shape[longest]] + spot[longest + 1:]
    return values.at[tuple(spot)].set(smallest).at[tuple(beside)].set(largest)


def steps_of(stream_key, dims, split, low, high):
    def one(position, parts):
        draws = jax.random.uniform(jax.random.fold_in(jax.random.fold_in(stream_key, 6), position), (parts,), jnp.float32, low / len(split), high / len(split))
        return jnp.repeat(jnp.exp(draws), dims[position] // parts).reshape((-1,) + (1,) * (len(dims) - position - 1))

    loudness = one(*split[0])
    for cut in split[1:]:
        loudness = loudness * one(*cut)
    return loudness


def noise(rng, dims, spread, limit, cuts=(), dtype=jnp.bfloat16):
    values = spread * jax.random.normal(rng, dims, jnp.float32)
    if cuts:
        values = values * steps_of(rng, dims, cuts, -0.22, 0.18)
    return jnp.clip(values, -limit, limit).astype(dtype)


def setup_inputs(seed: int = 0) -> dict:
    key_list = jax.random.split(jax.random.key(seed), 13)
    feats = noise(key_list[0], (CAMS, ROWS, COLS, C), 1.0, 6.0, ((0, 4), (1, 32)))
    cotangent = noise(key_list[1], (CAMS, ROWS, COLS, C), 1.0, 6.0, ((0, 4), (1, 32)))
    conv_w = noise(key_list[2], (9, GROUPS, CG, CG), (9 * CG) ** -0.5, 0.375)
    conv_b = noise(key_list[3], (C,), 0.5, 3.0, (), jnp.float32)
    w_query = draw_w_query(jax.random.fold_in(key_list[12], 71), 0)
    w_key = draw_w_key(jax.random.fold_in(key_list[12], 71), 0)
    w_value = noise(key_list[6], (C, ATT), C ** -0.5, 0.375)
    w_out = noise(key_list[7], (ATT, C), ATT ** -0.5, 0.375)
    time_table = noise(key_list[8], (FRAMES, C), 1.0, 6.0)
    frame_index = with_ends(jax.random.randint(key_list[9], (CAMS,), 0, FRAMES), jax.random.fold_in(key_list[9], 1), 0, FRAMES - 1).astype(jnp.int32)
    block_start = draw_block_start(jax.random.fold_in(key_list[12], 71), 0)
    block_count = draw_block_count(jax.random.fold_in(key_list[12], 71), 0)
    return {"feats": feats, "cotangent": cotangent, "conv_w": conv_w, "conv_b": conv_b, "w_query": w_query, "w_key": w_key, "w_value": w_value, "w_out": w_out, "time_table": time_table, "frame_index": frame_index, "block_start": block_start, "block_count": block_count}


def gelu_tanh(value):
    return 0.5 * value * (1.0 + jnp.tanh(0.7978845608028654 * (value + 0.044715 * value * value * value)))

def conv_taps(padded, weight, rows, cols):
    groups, width = (weight.shape[1], weight.shape[2])
    total = jnp.zeros((rows, cols, groups, width), jnp.float32)
    for tap in range(9):
        window = padded[tap // 3:tap // 3 + rows, tap % 3:tap % 3 + cols].reshape(rows, cols, groups, width)
        total = total + jnp.einsum('rwgi,gio->rwgo', window.astype(jnp.float32), weight[tap].astype(jnp.float32))
    return total.reshape(rows, cols, groups * width)

def conv_back(slope, weight, rows, cols):
    groups, width = (weight.shape[1], weight.shape[2])
    shaped = slope.astype(jnp.float32).reshape(rows, cols, groups, width)
    result = jnp.zeros((rows + 2, cols + 2, groups * width), jnp.float32)
    for tap in range(9):
        term = jnp.einsum('rwgo,gio->rwgi', shaped, weight[tap].astype(jnp.float32))
        result = result.at[tap // 3:tap // 3 + rows, tap % 3:tap % 3 + cols].add(term.reshape(rows, cols, groups * width))
    return result

def weight_grad(padded, slope, rows, cols, groups, width):
    shaped = slope.astype(jnp.float32).reshape(rows, cols, groups, width)
    taps = []
    for tap in range(9):
        window = padded[tap // 3:tap // 3 + rows, tap % 3:tap % 3 + cols].reshape(rows, cols, groups, width)
        taps.append(jnp.einsum('rwgi,rwgo->gio', window.astype(jnp.float32), shaped))
    return jnp.stack(taps)

def attend(queries, out_grad, keys, values, live):
    count, width = queries.shape
    heads = width // HEAD_DIM
    scale = 1.0 / math.sqrt(HEAD_DIM)
    query_heads = queries.astype(jnp.float32).reshape(count, heads, HEAD_DIM)
    key_heads = keys.astype(jnp.float32).reshape(-1, heads, HEAD_DIM)
    value_heads = values.astype(jnp.float32).reshape(-1, heads, HEAD_DIM)
    grad_heads = out_grad.astype(jnp.float32).reshape(count, heads, HEAD_DIM)
    scores = jnp.einsum('qhd,khd->hqk', query_heads, key_heads) * scale
    highest = lax.optimization_barrier(jnp.max(jnp.where(live, scores, -jnp.inf), axis=2, keepdims=True))
    unnormed = jnp.where(live, jnp.exp(scores - highest), 0.0)
    probs = unnormed / lax.optimization_barrier(jnp.sum(unnormed, axis=2, keepdims=True))
    probs_b = probs.astype(jnp.bfloat16).astype(jnp.float32)
    mixed = jnp.einsum('hqk,khd->qhd', probs_b, value_heads)
    delta = lax.optimization_barrier(jnp.sum(grad_heads * mixed, axis=2))
    prob_grad = jnp.einsum('qhd,khd->hqk', grad_heads, value_heads)
    score_grad = (probs * (prob_grad - delta.T[:, :, None]) * scale).astype(jnp.bfloat16).astype(jnp.float32)
    query_grad = jnp.einsum('hqk,khd->qhd', score_grad, key_heads)
    key_grad = jnp.einsum('hqk,qhd->khd', score_grad, query_heads)
    value_grad = jnp.einsum('hqk,qhd->khd', probs_b, grad_heads)
    return (query_grad.reshape(count, width), key_grad.reshape(-1, width), value_grad.reshape(-1, width))

def reference(feats, cotangent, conv_w, conv_b, w_query, w_key, w_value, w_out, time_table, frame_index, block_start, block_count):
    cams, rows, cols, chans = feats.shape
    groups, group_width = (conv_w.shape[1], conv_w.shape[2])
    width = w_query.shape[1]
    strips = rows // RS
    tokens = RS * cols
    blocks = tokens // BLK
    factor = 1.0 / math.sqrt(cams * rows * cols)
    conv_parts = []
    grad_w = jnp.zeros(conv_w.shape, jnp.float32)
    grad_b = jnp.zeros((chans,), jnp.float32)
    for camera in range(cams):
        padded = jnp.pad(feats[camera], ((1, 1), (1, 1), (0, 0)))
        summed = conv_taps(padded, conv_w, rows, cols) + conv_b
        slope = jax.vjp(gelu_tanh, summed)[1](cotangent[camera].astype(jnp.float32))[0]
        slope_b = slope.astype(jnp.bfloat16)
        back = conv_back(slope_b, conv_w, rows, cols)
        conv_parts.append(back[1:-1, 1:-1])
        grad_w = grad_w + weight_grad(padded, slope_b, rows, cols, groups, group_width)
        grad_b = grad_b + lax.optimization_barrier(jnp.sum(slope, axis=(0, 1)))
    conv_grad = jnp.stack(conv_parts)
    strip_feats = feats.reshape(cams, strips, tokens, chans).astype(jnp.float32)
    strip_cot = cotangent.reshape(cams, strips, tokens, chans).astype(jnp.float32)
    query = jnp.einsum('cstx,xy->csty', strip_feats, w_query.astype(jnp.float32)).astype(jnp.bfloat16)
    out_grad = jnp.einsum('cstx,yx->csty', strip_cot, w_out.astype(jnp.float32)).astype(jnp.bfloat16)
    frames = time_table[frame_index].astype(jnp.float32)
    key_input = (strip_feats + frames[:, None, None, :]).astype(jnp.bfloat16).astype(jnp.float32)
    keys = jnp.einsum('cstx,xy->csty', key_input, w_key.astype(jnp.float32)).astype(jnp.bfloat16)
    values = jnp.einsum('cstx,xy->csty', key_input, w_value.astype(jnp.float32)).astype(jnp.bfloat16)
    keys = keys.reshape(cams, strips, blocks, BLK, width)
    values = values.reshape(cams, strips, blocks, BLK, width)
    lanes = jnp.arange(3).astype(jnp.int32)
    slots = jnp.arange(MOSTB).astype(jnp.int32)

    def receive(index):
        view = index // strips
        strip = index % strips
        order = ((view + 1 + jnp.arange(cams - 1).astype(jnp.int32)) % cams).astype(jnp.int32)
        source_strip = strip - 1 + lanes
        inside = (source_strip >= 0) & (source_strip < strips)
        clipped = jnp.clip(source_strip, 0, strips - 1).astype(jnp.int32)
        target_lane = (2 - lanes)[:, None]
        start = block_start[order[None, :], clipped[:, None], view, target_lane]
        number = block_count[order[None, :], clipped[:, None], view, target_lane] * inside[:, None].astype(jnp.int32)
        block = (start[:, :, None] + slots).astype(jnp.int32)
        live = slots < number[:, :, None]
        picked_keys = keys[order[None, :, None], clipped[:, None, None], block].reshape(-1, width)
        picked_values = values[order[None, :, None], clipped[:, None, None], block].reshape(-1, width)
        live_tok = jnp.broadcast_to(live[..., None], live.shape + (BLK,)).reshape(-1)
        query_grad, key_grad, value_grad = attend(query[view, strip], out_grad[view, strip], picked_keys, picked_values, live_tok)
        key_b = key_grad.astype(jnp.bfloat16)
        value_b = value_grad.astype(jnp.bfloat16)
        slot_grad = jnp.dot(key_b, w_key.T, preferred_element_type=jnp.float32) + jnp.dot(value_b, w_value.T, preferred_element_type=jnp.float32)
        slot_grad = slot_grad.reshape(3, cams - 1, MOSTB, BLK, chans) * live[..., None, None].astype(jnp.float32)
        return (query_grad, slot_grad, order, clipped, block)
    index_all = jnp.arange(cams * strips).astype(jnp.int32)
    query_all, slot_all, order_all, clip_all, block_all = lax.map(receive, index_all)
    cam_index = jnp.broadcast_to(order_all[:, None, :, None], block_all.shape)
    strip_index = jnp.broadcast_to(clip_all[:, :, None, None], block_all.shape)
    input_grad = jnp.zeros((cams, strips, blocks, BLK, chans), jnp.float32).at[cam_index, strip_index, block_all].add(slot_all)
    query_term = jnp.dot(query_all.reshape(-1, width).astype(jnp.bfloat16), w_query.T, preferred_element_type=jnp.float32)
    attention_grad = query_term.reshape(cams, rows, cols, chans) + input_grad.reshape(cams, rows, cols, chans)
    grad_feats = (cotangent.astype(jnp.float32) + conv_grad + attention_grad).astype(jnp.bfloat16)
    return (grad_feats, grad_w * factor, grad_b * factor)
```

```python
import functools
import math

import jax
import jax.numpy as jnp
from jax import lax
from jax.experimental import pallas as pl
from jax.experimental.pallas import tpu as pltpu
from jax.sharding import Mesh
from jax.sharding import PartitionSpec as P

F32 = jnp.float32
BF16 = jnp.bfloat16
BLK = 128
PAIR = 2 * BLK
HEAD_DIM = 64
LANES = 128
DEAD = -1e30
VMEM = pl.BlockSpec(memory_space=pltpu.VMEM)
SMEM = pl.BlockSpec(memory_space=pltpu.SMEM)
HBM = pl.BlockSpec(memory_space=pl.ANY)
BIG = pltpu.CompilerParams(vmem_limit_bytes=56 << 20)


def dot(a, b):
    return jnp.dot(a, b, preferred_element_type=F32)


def dot_t(a, b):
    return lax.dot_general(a, b, (((1,), (1,)), ((), ())), preferred_element_type=F32)


def entry(source_view, source_strip, view, offset):
    return ((source_view * 32 + source_strip) * 4 + view) * 3 + offset


def offset_of(other, low):
    return 1 + other - low


def pack_kernel(place_ref, start_ref, flat_ref, near_ref, far_ref, sem):
    camera, strip = place_ref[0], place_ref[1]
    low = lax.rem(strip, 2)
    copies = []
    for view in range(4):
        for other in range(2):
            start = start_ref[entry(camera, strip, view, offset_of(other, low))]
            copies.append((start, near_ref.at[2 * view + other]))
    for shift in range(3):
        view = lax.rem(camera + 1 + shift, 4)
        start = start_ref[entry(camera, strip, view, 2 * low)]
        copies.append((start, far_ref.at[shift]))
    made = []
    for i, (start, target) in enumerate(copies):
        rows = pl.ds(pl.multiple_of(start * BLK, BLK), PAIR)
        made.append(pltpu.make_async_copy(flat_ref.at[rows], target, sem.at[i]))
        made[-1].start()
    for copy in made:
        copy.wait()


def project_kernel(flat_ref, grad_ref, wq_ref, wo_ref, query_ref, out_ref):
    query = dot(flat_ref[...], wq_ref[...]).astype(BF16)
    query_ref[...] = query * BF16(1.0 / math.sqrt(HEAD_DIM))
    out_ref[...] = dot_t(grad_ref[...], wo_ref[...]).astype(BF16)


def spread(rows_ref, tap):
    block = rows_ref[tap * 256 : (tap + 1) * 256, :]
    width = block.shape[1]
    pick = lax.broadcasted_iota(jnp.int32, (width, 256), 1) % width
    same = pick == lax.broadcasted_iota(jnp.int32, (width, 256), 0)
    tiled = dot(block, same.astype(F32).astype(BF16))
    row = lax.broadcasted_iota(jnp.int32, (256, 256), 0) // width
    lane = lax.broadcasted_iota(jnp.int32, (256, 256), 1) // width
    return jnp.where(row == lane, tiled, 0.0).astype(BF16)


def shifted(row):
    cols = row.shape[0]
    wide = row.astype(F32)
    column = lax.broadcasted_iota(jnp.int32, wide.shape, 0)
    before = jnp.where(column == 0, 0.0, pltpu.roll(wide, 1, 0))
    after = jnp.where(column == cols - 1, 0.0, pltpu.roll(wide, cols - 1, 0))
    return before.astype(BF16), row, after.astype(BF16)


def fill_padded(pad_ref, top_ref, flat_ref, bottom_ref, cols, rows):
    for r in range(rows + 2):
        if r == 0:
            line = top_ref[...]
        elif r == rows + 1:
            line = bottom_ref[...]
        else:
            line = flat_ref[(r - 1) * cols : r * cols, :]
        for dx, part in enumerate(shifted(line)):
            pad_ref[r * cols : (r + 1) * cols, dx * 256 : (dx + 1) * 256] = part


def conv_kernel(
    flat_ref, top_ref, bottom_ref, grad_ref, w_ref, b_ref, slope_ref, sums_ref, pad_ref, wide_ref, turn_ref
):
    cols = top_ref.shape[0]
    rows = flat_ref.shape[0] // cols
    fill_padded(pad_ref, top_ref, flat_ref, bottom_ref, cols, rows)
    for tap in range(9):
        wide_ref[tap * 256 : (tap + 1) * 256, :] = spread(w_ref, tap)
    bias_sum = jnp.zeros((1, 256), F32)
    for r in range(rows):
        act = b_ref[...]
        for dy in range(3):
            act = act + dot(
                pad_ref[(r + dy) * cols : (r + dy + 1) * cols, :], wide_ref[dy * 768 : (dy + 1) * 768, :]
            )
        square = act * act
        bent = jnp.tanh(0.7978845608028654 * (act + 0.044715 * square * act))
        inner = 0.7978845608028654 * (1.0 + 3.0 * 0.044715 * square)
        gain = 0.5 * (1.0 + bent) + 0.5 * act * (1.0 - bent * bent) * inner
        slope = grad_ref[r * cols : (r + 1) * cols, :].astype(F32) * gain
        bias_sum = bias_sum + jnp.sum(slope, axis=0, keepdims=True)
        slope_b = slope.astype(BF16)
        slope_ref[r * cols : (r + 1) * cols, :] = slope_b
        turn_ref[:, r * cols : (r + 1) * cols] = slope_b.T
    lane_group = lax.broadcasted_iota(jnp.int32, (32, LANES), 1) // 32
    for dy in range(3):
        full = dot(turn_ref[...], pad_ref[dy * cols : (dy + rows) * cols, :])
        for dx in range(3):
            for half in range(2):
                part = full[half * LANES : (half + 1) * LANES, dx * 256 + half * LANES : dx * 256 + (half + 1) * LANES]
                packed = jnp.zeros((32, LANES), F32)
                for g in range(4):
                    packed = packed + jnp.where(lane_group == g, part[g * 32 : (g + 1) * 32, :], 0.0)
                at = ((3 * dy + dx) * 2 + half) * 32
                sums_ref[at : at + 32, :] = packed
    tail = sums_ref.shape[0] - 576
    first = lax.broadcasted_iota(jnp.int32, (tail, LANES), 0)
    sums_ref[576:, :] = jnp.where(first == 0, bias_sum[:, :LANES], 0.0) + jnp.where(
        first == 1, bias_sum[:, LANES:], 0.0
    )


def back_kernel(slope_ref, top_ref, bottom_ref, grad_ref, w_ref, base_ref, pad_ref, wide_ref):
    cols = top_ref.shape[0]
    rows = slope_ref.shape[0] // cols
    fill_padded(pad_ref, top_ref, slope_ref, bottom_ref, cols, rows)
    for tap in range(9):
        dy, dx = tap // 3, tap % 3
        wide_ref[dy * 256 : (dy + 1) * 256, (2 - dx) * 256 : (3 - dx) * 256] = spread(w_ref, tap)
    for r in range(rows):
        total = grad_ref[r * cols : (r + 1) * cols, :].astype(F32)
        for dy in range(3):
            total = total + dot_t(
                pad_ref[(r + 2 - dy) * cols : (r + 3 - dy) * cols, :], wide_ref[dy * 256 : (dy + 1) * 256, :]
            )
        base_ref[r * cols : (r + 1) * cols, :] = total


def attend_kernel(
    place_ref,
    frame_ref,
    count_ref,
    near_ref,
    far_ref,
    table_ref,
    query_ref,
    grad_ref,
    wk_ref,
    wv_ref,
    wq_ref,
    base_ref,
    near_out_ref,
    far_out_ref,
    part_ref,
    key_s,
    value_s,
    turn_s,
    key_grad_s,
    value_grad_s,
    score_s,
    pull_s,
    *,
    span,
):
    camera, strip = place_ref[0], place_ref[1]
    low = lax.rem(strip, 2)
    pair = strip - low
    far_strip = strip + 2 * low - 1
    inside = jnp.logical_and(far_strip >= 0, far_strip < 32)
    far_safe = jnp.clip(far_strip, 0, 31)
    tokens = query_ref.shape[0]
    groups = []
    for shift in range(3):
        view = lax.rem(camera + 1 + shift, 4)
        for other in range(2):
            count = count_ref[entry(view, pair + other, camera, offset_of(low, other))]
            groups.append((near_ref, near_out_ref, 2 * view + other, view, count))
    for shift in range(3):
        view = lax.rem(camera + 3 - shift, 4)
        count = jnp.where(inside, count_ref[entry(view, far_safe, camera, 2 - 2 * low)], 0)
        groups.append((far_ref, far_out_ref, shift, view, count))
    biases = []
    for i, (source, _, slot, view, count) in enumerate(groups):
        rows = slice(i * PAIR, (i + 1) * PAIR)
        embed = table_ref[pl.ds(frame_ref[view], 1), :]
        entering = (source[slot].astype(F32) + embed).astype(BF16)
        keys = dot(entering, wk_ref[...]).astype(BF16)
        key_s[rows, :] = keys
        value_s[rows, :] = dot(entering, wv_ref[...]).astype(BF16)
        turn_s[:, rows] = keys.T
        biases += [jnp.where(count > b, 0.0, DEAD).astype(F32) for b in range(2)]
    key_grad_s[...] = jnp.zeros_like(key_grad_s)
    value_grad_s[...] = jnp.zeros_like(value_grad_s)
    first_head = lax.broadcasted_iota(jnp.int32, (span, LANES), 1) < HEAD_DIM
    both = 2 * span

    def tile(t, carry):
        here = pl.ds(pl.multiple_of(t * span, span), span)
        found = []
        for p in range(2):
            lanes = slice(p * LANES, (p + 1) * LANES)
            query, grad = query_ref[here, lanes], grad_ref[here, lanes]
            zero = jnp.zeros_like(query)
            queries = jnp.concatenate(
                [jnp.where(first_head, query, zero), jnp.where(first_head, zero, query)], 0
            )
            grads = jnp.concatenate(
                [jnp.where(first_head, grad, zero), jnp.where(first_head, zero, grad)], 0
            )
            highest = None
            for c, bias in enumerate(biases):
                rows = slice(c * BLK, (c + 1) * BLK)
                scores = dot_t(key_s[rows, lanes], queries)
                score_s[p, rows, :] = scores
                top = jnp.max(scores.reshape(BLK // 8, 8, both), 0) + bias
                highest = top if c == 0 else jnp.maximum(highest, top)
            highest = jnp.max(highest, 0, keepdims=True)
            norm, delta = 0.0, 0.0
            for c, bias in enumerate(biases):
                rows = slice(c * BLK, (c + 1) * BLK)
                weight = jnp.exp(score_s[p, rows, :] - (highest - bias))
                score_s[p, rows, :] = weight
                pull = dot_t(value_s[rows, lanes], grads)
                pull_s[p, rows, :] = pull
                norm = norm + jnp.sum(weight.reshape(BLK // 8, 8, both), 0)
                delta = delta + jnp.sum((weight * pull).reshape(BLK // 8, 8, both), 0)
            inverse = 1.0 / jnp.sum(norm, 0, keepdims=True)
            delta = jnp.sum(delta, 0, keepdims=True) * inverse
            upper, lower = 0.0, 0.0
            for c in range(len(biases)):
                rows = slice(c * BLK, (c + 1) * BLK)
                probs = score_s[p, rows, :] * inverse
                score_grad = (probs * (pull_s[p, rows, :] - delta)).astype(BF16)
                key_grad_s[rows, lanes] += dot(score_grad, queries)
                value_grad_s[rows, lanes] += dot(probs.astype(BF16), grads)
                head = p * LANES
                upper = upper + dot(turn_s[head : head + HEAD_DIM, rows], score_grad[:, :span])
                lower = lower + dot(turn_s[head + HEAD_DIM : head + LANES, rows], score_grad[:, span:])
            found += [upper, lower]
        query_grad = (jnp.concatenate(found, 0) * (1.0 / math.sqrt(HEAD_DIM))).T.astype(BF16)
        part_ref[here, :] = base_ref[here, :] + dot_t(query_grad, wq_ref[...])
        return carry

    lax.fori_loop(0, tokens // span, tile, 0)
    for i, (_, target, slot, _, _) in enumerate(groups):
        rows = slice(i * PAIR, (i + 1) * PAIR)
        sent = dot_t(key_grad_s[rows, :].astype(BF16), wk_ref[...])
        sent = sent + dot_t(value_grad_s[rows, :].astype(BF16), wv_ref[...])
        target[slot] = sent.astype(BF16)


def join_kernel(place_ref, start_ref, part_ref, near_ref, far_ref, out_ref, total_s):
    camera, strip = place_ref[0], place_ref[1]
    low = lax.rem(strip, 2)
    total_s[...] = part_ref[...]

    def add(start, block):
        rows = pl.ds(pl.multiple_of(start * BLK, BLK), PAIR)
        total_s[rows, :] += block.astype(F32)

    for shift in range(3):
        view = lax.rem(camera + 1 + shift, 4)
        for other in range(2):
            add(start_ref[entry(camera, strip, view, offset_of(other, low))], near_ref[2 * view + other])
        add(start_ref[entry(camera, strip, view, 2 * low)], far_ref[shift])
    out_ref[...] = total_s[...].astype(BF16)


def sum_kernel(pieces_ref, out_ref):
    out_ref[...] = jnp.broadcast_to(jnp.sum(pieces_ref[...], 0, keepdims=True), out_ref.shape)


def finish_kernel(sums_ref, w_ref, b_ref, *, factor):
    for block in range(18):
        part = sums_ref[block * 32 : (block + 1) * 32, :] * factor
        w_ref[block * LANES : (block + 1) * LANES, :] = part.T
    b_ref[:, :LANES] = sums_ref[576:577, :] * factor
    b_ref[:, LANES:] = sums_ref[577:578, :] * factor


def call(kernel, name, out, ins, outs, scratch=(), **options):
    return pl.pallas_call(
        functools.partial(kernel, **options),
        out_shape=out,
        in_specs=ins,
        out_specs=outs,
        scratch_shapes=list(scratch),
        compiler_params=BIG,
        name=name,
    )


def shape(dims, kind):
    return jax.ShapeDtypeStruct(dims, kind)


ALL = ("cam", "pair", "low")
RING = ("cam", "low")


def place(camera, strip):
    return camera * 32 + strip


def neighbours(step):
    return [
        (place(c, s), place(c, s + step)) for c in range(4) for s in range(32) if 0 <= s + step < 32
    ]


def far_pairs(shift):
    pairs = []
    for c in range(4):
        for s in range(32):
            other = s + 1 if s % 2 else s - 1
            if 0 <= other < 32:
                pairs.append((place(c, s), place((c + shift) % 4, other)))
    return pairs


def exchange(block):
    return lax.all_to_all(block, RING, split_axis=0, concat_axis=0, tiled=True)


def shards(
    feats,
    cotangent,
    conv_w,
    conv_b,
    w_query,
    w_key,
    w_value,
    w_out,
    time_table,
    frame_index,
    block_start,
    block_count,
):
    rows, cols, chans = feats.shape[1:]
    tokens = rows * cols
    keys = 9 * PAIR
    camera = lax.axis_index("cam")
    strip = 2 * lax.axis_index("pair") + lax.axis_index("low")
    where = jnp.stack([camera, strip]).astype(jnp.int32)
    flat = feats.reshape(tokens, chans)
    grad_flat = cotangent.reshape(tokens, chans)
    starts = block_start.reshape(-1)
    counts = block_count.reshape(-1)
    taps = conv_w.reshape(-1, conv_w.shape[-1])

    near, far = call(
        pack_kernel,
        "pack",
        (shape((8, PAIR, chans), BF16), shape((3, PAIR, chans), BF16)),
        [SMEM, SMEM, HBM],
        (HBM, HBM),
        [pltpu.SemaphoreType.DMA((11,))],
    )(where, starts, flat)
    top = lax.ppermute(flat[tokens - cols :], ALL, neighbours(1))
    bottom = lax.ppermute(flat[:cols], ALL, neighbours(-1))
    near = exchange(near)
    far = jnp.stack([lax.ppermute(far[i], ALL, far_pairs(i + 1)) for i in range(3)])

    query, out_grad = call(
        project_kernel,
        "project",
        (shape((tokens, chans), BF16), shape((tokens, chans), BF16)),
        [VMEM] * 4,
        (VMEM, VMEM),
    )(flat, grad_flat, w_query, w_out)

    slope, sums = call(
        conv_kernel,
        "conv",
        (shape((tokens, chans), BF16), shape((1024, LANES), F32)),
        [VMEM] * 6,
        (VMEM, VMEM),
        [
            pltpu.VMEM(((rows + 2) * cols, 3 * chans), BF16),
            pltpu.VMEM((9 * chans, chans), BF16),
            pltpu.VMEM((chans, tokens), BF16),
        ],
    )(flat, top, bottom, grad_flat, taps, conv_b.reshape(1, chans))

    slope_top = lax.ppermute(slope[tokens - cols :], ALL, neighbours(1))
    slope_bottom = lax.ppermute(slope[:cols], ALL, neighbours(-1))

    pieces = lax.all_to_all(sums.reshape(128, 8, LANES), ALL, split_axis=0, concat_axis=0, tiled=True)
    pieces = call(sum_kernel, "add_pieces", shape((128, 8, LANES), F32), [VMEM], VMEM)(pieces)
    summed = lax.all_to_all(pieces, ALL, split_axis=0, concat_axis=0, tiled=True)
    total_w, total_b = call(
        finish_kernel,
        "finish",
        (shape((9 * chans, 32), F32), shape((1, chans), F32)),
        [VMEM],
        (VMEM, VMEM),
        factor=1.0 / math.sqrt(4 * 96 * 512),
    )(summed.reshape(1024, LANES))

    base = call(
        back_kernel,
        "back",
        shape((tokens, chans), F32),
        [VMEM] * 5,
        VMEM,
        [
            pltpu.VMEM(((rows + 2) * cols, 3 * chans), BF16),
            pltpu.VMEM((3 * chans, 3 * chans), BF16),
        ],
    )(slope, slope_top, slope_bottom, grad_flat, taps)

    span = 256
    near_grad, far_grad, part = call(
        attend_kernel,
        "attend",
        (
            shape((8, PAIR, chans), BF16),
            shape((3, PAIR, chans), BF16),
            shape((tokens, chans), F32),
        ),
        [SMEM, SMEM, SMEM] + [VMEM] * 9,
        (VMEM, VMEM, VMEM),
        [
            pltpu.VMEM((keys, chans), BF16),
            pltpu.VMEM((keys, chans), BF16),
            pltpu.VMEM((chans, keys), BF16),
            pltpu.VMEM((keys, chans), F32),
            pltpu.VMEM((keys, chans), F32),
            pltpu.VMEM((2, keys, 2 * span), F32),
            pltpu.VMEM((2, keys, 2 * span), F32),
        ],
        span=span,
    )(
        where,
        frame_index,
        counts,
        near,
        far,
        time_table.astype(F32),
        query,
        out_grad,
        w_key,
        w_value,
        w_query,
        base,
    )
    near_back = exchange(near_grad)
    far_back = jnp.stack([lax.ppermute(far_grad[i], ALL, far_pairs(-i - 1)) for i in range(3)])
    grad_feats = call(
        join_kernel,
        "join",
        shape((tokens, chans), BF16),
        [SMEM, SMEM, VMEM, VMEM, VMEM],
        VMEM,
        [pltpu.VMEM((tokens, chans), F32)],
    )(where, starts, part, near_back, far_back)
    return (
        grad_feats.reshape(1, rows, cols, chans),
        total_w.reshape(conv_w.shape),
        total_b.reshape(chans),
    )


def solution(mesh):
    split = Mesh(mesh.devices.reshape(4, 16, 2), ALL)
    whole = P("cam", ("pair", "low"), None, None)
    return jax.shard_map(
        shards,
        mesh=split,
        in_specs=(whole, whole) + (P(),) * 10,
        out_specs=(whole, P(), P()),
        check_vma=False,
    )
```

```python
import functools
import math

import jax
import jax.numpy as jnp
from jax import lax
from jax.experimental import pallas as pl
from jax.experimental.pallas import tpu as pltpu
from jax.sharding import Mesh
from jax.sharding import PartitionSpec as P

F32 = jnp.float32
BF16 = jnp.bfloat16
BLK = 128
PAIR = 2 * BLK
HEAD_DIM = 64
LANES = 128
DEAD = -1e30
HALF = 296
VMEM = pl.BlockSpec(memory_space=pltpu.VMEM)
SMEM = pl.BlockSpec(memory_space=pltpu.SMEM)
BIG = pltpu.CompilerParams(vmem_limit_bytes=56 << 20)


def dot(a, b):
    return jnp.dot(a, b, preferred_element_type=F32)


def dot_t(a, b):
    return lax.dot_general(a, b, (((1,), (1,)), ((), ())), preferred_element_type=F32)


def entry(source_view, source_strip, view, offset):
    return ((source_view * 32 + source_strip) * 4 + view) * 3 + offset


def row_of(block):
    return block // 9 * HALF + block % 9 * 32


def start_of(table_ref, at):
    return lax.shift_right_logical(table_ref[at], 2)


def count_of(table_ref, at):
    return lax.bitwise_and(table_ref[at], 3)


def offset_of(other, low):
    return 1 + other - low


def pack_kernel(place_ref, table_ref, flat_ref, near_ref, far0_ref, far1_ref, far2_ref):
    camera, strip = place_ref[0], place_ref[1]
    low = lax.rem(strip, 2)

    def blocks(view, offset):
        start = start_of(table_ref, entry(camera, strip, view, offset))
        return flat_ref[pl.ds(pl.multiple_of(start * BLK, BLK), PAIR), :]

    for view in range(4):
        for other in range(2):
            near_ref[2 * view + other] = blocks(view, offset_of(other, low))
    for shift, far_ref in enumerate((far0_ref, far1_ref, far2_ref)):
        far_ref[...] = blocks(lax.rem(camera + 1 + shift, 4), 2 * low)


def project_kernel(flat_ref, grad_ref, wq_ref, wo_ref, query_ref, out_ref):
    query = dot(flat_ref[...], wq_ref[...]).astype(BF16)
    query_ref[...] = query * BF16(1.0 / math.sqrt(HEAD_DIM))
    out_ref[...] = dot_t(grad_ref[...], wo_ref[...]).astype(BF16)


def spread(rows_ref, tap):
    block = rows_ref[tap * 256 : (tap + 1) * 256, :]
    width = block.shape[1]
    pick = lax.broadcasted_iota(jnp.int32, (width, 256), 1) % width
    same = pick == lax.broadcasted_iota(jnp.int32, (width, 256), 0)
    tiled = dot(block, same.astype(F32).astype(BF16))
    row = lax.broadcasted_iota(jnp.int32, (256, 256), 0) // width
    lane = lax.broadcasted_iota(jnp.int32, (256, 256), 1) // width
    return jnp.where(row == lane, tiled, 0.0).astype(BF16)


def shifted(row):
    cols = row.shape[0]
    wide = row.astype(F32)
    column = lax.broadcasted_iota(jnp.int32, wide.shape, 0)
    before = jnp.where(column == 0, 0.0, pltpu.roll(wide, 1, 0))
    after = jnp.where(column == cols - 1, 0.0, pltpu.roll(wide, cols - 1, 0))
    return before.astype(BF16), row, after.astype(BF16)


def fill_padded(place_ref, pad_ref, top_ref, flat_ref, bottom_ref, cols, rows):
    strip = place_ref[1]
    for r in range(rows + 2):
        if r == 0:
            line = jnp.where(strip > 0, top_ref[...], 0)
        elif r == rows + 1:
            line = jnp.where(strip < 31, bottom_ref[...], 0)
        else:
            line = flat_ref[(r - 1) * cols : r * cols, :]
        for dx, part in enumerate(shifted(line)):
            pad_ref[r * cols : (r + 1) * cols, dx * 256 : (dx + 1) * 256] = part


def conv_kernel(
    place_ref, flat_ref, top_ref, bottom_ref, grad_ref, w_ref, b_ref, slope_ref, first_ref, last_ref, sums_ref, pad_ref, wide_ref, turn_ref
):
    cols = top_ref.shape[0]
    rows = flat_ref.shape[0] // cols
    fill_padded(place_ref, pad_ref, top_ref, flat_ref, bottom_ref, cols, rows)
    for tap in range(9):
        wide_ref[tap * 256 : (tap + 1) * 256, :] = spread(w_ref, tap)
    bias_sum = jnp.zeros((1, 256), F32)
    for r in range(rows):
        act = b_ref[...]
        for dy in range(3):
            act = act + dot(
                pad_ref[(r + dy) * cols : (r + dy + 1) * cols, :], wide_ref[dy * 768 : (dy + 1) * 768, :]
            )
        square = act * act
        bent = jnp.tanh(0.7978845608028654 * (act + 0.044715 * square * act))
        inner = 0.7978845608028654 * (1.0 + 3.0 * 0.044715 * square)
        gain = 0.5 * (1.0 + bent) + 0.5 * act * (1.0 - bent * bent) * inner
        slope = grad_ref[r * cols : (r + 1) * cols, :].astype(F32) * gain
        bias_sum = bias_sum + jnp.sum(slope, axis=0, keepdims=True)
        slope_b = slope.astype(BF16)
        slope_ref[r * cols : (r + 1) * cols, :] = slope_b
        turn_ref[:, r * cols : (r + 1) * cols] = slope_b.T
        if r == 0:
            first_ref[...] = slope_b
        if r == rows - 1:
            last_ref[...] = slope_b
    lane_group = lax.broadcasted_iota(jnp.int32, (32, LANES), 1) // 32
    for dy in range(3):
        full = dot(turn_ref[...], pad_ref[dy * cols : (dy + rows) * cols, :])
        for dx in range(3):
            for half in range(2):
                part = full[half * LANES : (half + 1) * LANES, dx * 256 + half * LANES : dx * 256 + (half + 1) * LANES]
                packed = jnp.zeros((32, LANES), F32)
                for g in range(4):
                    packed = packed + jnp.where(lane_group == g, part[g * 32 : (g + 1) * 32, :], 0.0)
                at = row_of((3 * dy + dx) * 2 + half)
                sums_ref[at : at + 32, :] = packed
    sums_ref[2 * HALF :, :] = jnp.zeros((sums_ref.shape[0] - 2 * HALF, LANES), F32)
    for half in range(2):
        at = half * HALF + HALF - 8
        sums_ref[at : at + 8, :] = jnp.broadcast_to(bias_sum[:, half * LANES : (half + 1) * LANES], (8, LANES))


def back_kernel(place_ref, slope_ref, top_ref, bottom_ref, grad_ref, part_ref, w_ref, base_ref, pad_ref, wide_ref):
    cols = top_ref.shape[0]
    rows = slope_ref.shape[0] // cols
    fill_padded(place_ref, pad_ref, top_ref, slope_ref, bottom_ref, cols, rows)
    for tap in range(9):
        dy, dx = tap // 3, tap % 3
        wide_ref[dy * 256 : (dy + 1) * 256, (2 - dx) * 256 : (3 - dx) * 256] = spread(w_ref, tap)
    for r in range(rows):
        total = grad_ref[r * cols : (r + 1) * cols, :].astype(F32) + part_ref[r * cols : (r + 1) * cols, :]
        for dy in range(3):
            total = total + dot_t(
                pad_ref[(r + 2 - dy) * cols : (r + 3 - dy) * cols, :], wide_ref[dy * 256 : (dy + 1) * 256, :]
            )
        base_ref[r * cols : (r + 1) * cols, :] = total


def attend_kernel(
    place_ref,
    frame_ref,
    blocks_ref,
    near_ref,
    far0_ref,
    far1_ref,
    far2_ref,
    table_ref,
    query_ref,
    grad_ref,
    wk_ref,
    wv_ref,
    wq_ref,
    near_out_ref,
    far0_out_ref,
    far1_out_ref,
    far2_out_ref,
    part_ref,
    key_s,
    value_s,
    turn_s,
    key_grad_s,
    value_grad_s,
    score_s,
    pull_s,
    score_grad_s,
    probs_s,
    *,
    span,
):
    camera, strip = place_ref[0], place_ref[1]
    low = lax.rem(strip, 2)
    pair = strip - low
    far_strip = strip + 2 * low - 1
    inside = jnp.logical_and(far_strip >= 0, far_strip < 32)
    far_safe = jnp.clip(far_strip, 0, 31)
    tokens = query_ref.shape[0]
    groups = []
    for shift in range(3):
        view = lax.rem(camera + 1 + shift, 4)
        for other in range(2):
            count = count_of(blocks_ref, entry(view, pair + other, camera, offset_of(low, other)))
            groups.append((near_ref.at[2 * view + other], near_out_ref.at[2 * view + other], view, count))
    fars = ((far0_ref, far0_out_ref), (far1_ref, far1_out_ref), (far2_ref, far2_out_ref))
    for shift in range(3):
        view = lax.rem(camera + 3 - shift, 4)
        count = jnp.where(inside, count_of(blocks_ref, entry(view, far_safe, camera, 2 - 2 * low)), 0)
        groups.append(fars[shift] + (view, count))
    biases = []
    for i, (source, _, view, count) in enumerate(groups):
        rows = slice(i * PAIR, (i + 1) * PAIR)
        embed = table_ref[pl.ds(frame_ref[view], 1), :]
        entering = (source[...].astype(F32) + embed).astype(BF16)
        keys = dot(entering, wk_ref[...]).astype(BF16)
        key_s[rows, :] = keys
        value_s[rows, :] = dot(entering, wv_ref[...]).astype(BF16)
        turn_s[:, rows] = keys.T
        biases += [jnp.where(count > b, 0.0, DEAD).astype(F32) for b in range(2)]
    key_grad_s[...] = jnp.zeros_like(key_grad_s)
    value_grad_s[...] = jnp.zeros_like(value_grad_s)
    first_head = lax.broadcasted_iota(jnp.int32, (span, LANES), 1) < HEAD_DIM
    both = 2 * span

    def tile(t, carry):
        here = pl.ds(pl.multiple_of(t * span, span), span)
        found = []
        for p in range(2):
            lanes = slice(p * LANES, (p + 1) * LANES)
            query, grad = query_ref[here, lanes], grad_ref[here, lanes]
            zero = jnp.zeros_like(query)
            queries = jnp.concatenate(
                [jnp.where(first_head, query, zero), jnp.where(first_head, zero, query)], 0
            )
            grads = jnp.concatenate(
                [jnp.where(first_head, grad, zero), jnp.where(first_head, zero, grad)], 0
            )
            score_s[...] = dot_t(key_s[:, lanes], queries)
            pull_s[...] = dot_t(value_s[:, lanes], grads)
            chunks = [(slice(c * BLK, (c + 1) * BLK), bias) for c, bias in enumerate(biases)]
            highest = None
            for rows, bias in chunks:
                top = jnp.max(score_s[rows, :].reshape(BLK // 8, 8, both), 0) + bias
                highest = top if highest is None else jnp.maximum(highest, top)
            highest = jnp.max(highest, 0, keepdims=True)
            norm, delta = 0.0, 0.0
            for rows, bias in chunks:
                weight = jnp.exp(score_s[rows, :] - (highest - bias))
                norm = norm + jnp.sum(weight.reshape(BLK // 8, 8, both), 0)
                delta = delta + jnp.sum((weight * pull_s[rows, :]).reshape(BLK // 8, 8, both), 0)
            norm = jnp.sum(norm, 0, keepdims=True)
            delta = jnp.sum(delta, 0, keepdims=True) / norm
            level = highest + jnp.log(norm)
            for rows, bias in chunks:
                probs = jnp.exp(score_s[rows, :] - (level - bias))
                score_grad_s[rows, :] = (probs * (pull_s[rows, :] - delta)).astype(BF16)
                probs_s[rows, :] = probs.astype(BF16)
            key_grad_s[:, lanes] += dot(score_grad_s[...], queries)
            value_grad_s[:, lanes] += dot(probs_s[...], grads)
            head = p * LANES
            upper = dot(turn_s[head : head + HEAD_DIM, :], score_grad_s[:, :span])
            lower = dot(turn_s[head + HEAD_DIM : head + LANES, :], score_grad_s[:, span:])
            found += [upper, lower]
        query_grad = (jnp.concatenate(found, 0) * (1.0 / math.sqrt(HEAD_DIM))).T.astype(BF16)
        part_ref[here, :] = dot_t(query_grad, wq_ref[...])
        return carry

    lax.fori_loop(0, tokens // span, tile, 0)
    for i, (_, target, _, _) in enumerate(groups):
        rows = slice(i * PAIR, (i + 1) * PAIR)
        sent = dot_t(key_grad_s[rows, :].astype(BF16), wk_ref[...])
        sent = sent + dot_t(value_grad_s[rows, :].astype(BF16), wv_ref[...])
        target[...] = sent.astype(BF16)


def join_kernel(place_ref, table_ref, part_ref, near_ref, far0_ref, far1_ref, far2_ref, out_ref, total_s):
    camera, strip = place_ref[0], place_ref[1]
    low = lax.rem(strip, 2)
    total_s[...] = part_ref[...]

    def add(start, block):
        rows = pl.ds(pl.multiple_of(start * BLK, BLK), PAIR)
        total_s[rows, :] += block.astype(F32)

    for shift in range(3):
        view = lax.rem(camera + 1 + shift, 4)
        for other in range(2):
            add(start_of(table_ref, entry(camera, strip, view, offset_of(other, low))), near_ref[2 * view + other])
        add(start_of(table_ref, entry(camera, strip, view, 2 * low)), (far0_ref, far1_ref, far2_ref)[shift][...])
    out_ref[...] = total_s[...].astype(BF16)


def sum_kernel(pieces_ref, out_ref):
    out_ref[...] = jnp.broadcast_to(jnp.sum(pieces_ref[...], 0, keepdims=True), out_ref.shape)


def finish_kernel(sums_ref, w_ref, b_ref, *, factor):
    for block in range(18):
        at = row_of(block)
        w_ref[block * LANES : (block + 1) * LANES, :] = (sums_ref[at : at + 32, :] * factor).T
    b_ref[:, :LANES] = sums_ref[HALF - 8 : HALF - 7, :] * factor
    b_ref[:, LANES:] = sums_ref[2 * HALF - 8 : 2 * HALF - 7, :] * factor


def call(kernel, name, micros, out, ins, outs, scratch=(), **options):
    cost = pl.CostEstimate(flops=int(micros * 1e9), bytes_accessed=int(micros * 3e6), transcendentals=0)
    return pl.pallas_call(
        functools.partial(kernel, **options),
        out_shape=out,
        in_specs=ins,
        out_specs=outs,
        scratch_shapes=list(scratch),
        compiler_params=BIG,
        cost_estimate=cost,
        name=name,
    )


def shape(dims, kind):
    return jax.ShapeDtypeStruct(dims, kind)


ALL = ("high", "core", "x", "z", "low")
RING = ("high", "core", "low")


def place(camera, strip):
    return camera * 32 + strip


def neighbours(step):
    return [(place(c, s), place(c, (s + step) % 32)) for c in range(4) for s in range(32)]


def far_pairs(shift):
    return [
        (place(c, s), place((c + shift) % 4, (s + 1 if s % 2 else s - 1) % 32))
        for c in range(4)
        for s in range(32)
    ]


def exchange(block):
    return lax.all_to_all(block, RING, split_axis=0, concat_axis=0, tiled=True)


def shards(
    feats,
    cotangent,
    conv_w,
    conv_b,
    w_query,
    w_key,
    w_value,
    w_out,
    time_table,
    frame_index,
    block_start,
    block_count,
):
    rows, cols, chans = feats.shape[1:]
    tokens = rows * cols
    keys = 9 * PAIR
    core = lax.axis_index("core")
    camera = 2 * lax.axis_index("high") + core
    strip = 8 * lax.axis_index("x") + 2 * lax.axis_index("z") + lax.axis_index("low")
    where = jnp.stack([camera, strip]).astype(jnp.int32)
    flat = feats.reshape(tokens, chans)
    grad_flat = cotangent.reshape(tokens, chans)
    table = (block_start * 4 + block_count).reshape(-1)
    taps = conv_w.reshape(-1, conv_w.shape[-1])

    row = shape((cols, chans), BF16)
    slot = shape((PAIR, chans), BF16)
    slots = shape((8, PAIR, chans), BF16)
    top = lax.ppermute(flat[tokens - cols :], ALL, neighbours(1))
    bottom = lax.ppermute(flat[:cols], ALL, neighbours(-1))
    near, *far = call(
        pack_kernel,
        "pack",
        3,
        (slots, slot, slot, slot),
        [SMEM, SMEM, VMEM],
        (VMEM,) * 4,
    )(where, table, flat)
    flat_conv, near = lax.optimization_barrier((flat, near))
    near = exchange(near)
    far = [lax.ppermute(far[i], ALL, far_pairs(i + 1)) for i in range(3)]
    slope, slope_first, slope_last, sums = call(
        conv_kernel,
        "conv",
        8,
        (shape((tokens, chans), BF16), row, row, shape((1024, LANES), F32)),
        [SMEM] + [VMEM] * 6,
        (VMEM,) * 4,
        [
            pltpu.VMEM(((rows + 2) * cols, 3 * chans), BF16),
            pltpu.VMEM((9 * chans, chans), BF16),
            pltpu.VMEM((chans, tokens), BF16),
        ],
    )(where, flat_conv, top, bottom, grad_flat, taps, conv_b.reshape(1, chans))

    near, *far, sums, flat_next = lax.optimization_barrier((near, *far, sums, flat))
    pieces = lax.all_to_all(sums.reshape(128, 8, LANES), ALL, split_axis=0, concat_axis=0, tiled=True)
    query, out_grad = call(
        project_kernel,
        "project",
        3,
        (shape((tokens, chans), BF16), shape((tokens, chans), BF16)),
        [VMEM] * 4,
        (VMEM,) * 2,
    )(flat_next, grad_flat, w_query, w_out)
    pieces = call(sum_kernel, "add_pieces", 2, shape((128, 8, LANES), F32), [VMEM], VMEM)(pieces)
    pieces, near, query, slope_first, slope_last = lax.optimization_barrier(
        (pieces, near, query, slope_first, slope_last)
    )
    slope_top = lax.ppermute(slope_last, ALL, neighbours(1))
    slope_bottom = lax.ppermute(slope_first, ALL, neighbours(-1))
    summed = lax.all_to_all(pieces, ALL, split_axis=0, concat_axis=0, tiled=True)

    span = 256
    near_grad, *far_grad, part = call(
        attend_kernel,
        "attend",
        58,
        (
            slots,
            slot,
            slot,
            slot,
            shape((tokens, chans), F32),
        ),
        [SMEM, SMEM, SMEM] + [VMEM] * 10,
        (VMEM,) * 5,
        [
            pltpu.VMEM((keys, chans), BF16),
            pltpu.VMEM((keys, chans), BF16),
            pltpu.VMEM((chans, keys), BF16),
            pltpu.VMEM((keys, chans), F32),
            pltpu.VMEM((keys, chans), F32),
            pltpu.VMEM((keys, 2 * span), F32),
            pltpu.VMEM((keys, 2 * span), F32),
            pltpu.VMEM((keys, 2 * span), BF16),
            pltpu.VMEM((keys, 2 * span), BF16),
        ],
        span=span,
    )(
        where,
        frame_index,
        table,
        near,
        *far,
        time_table.astype(F32),
        query,
        out_grad,
        w_key,
        w_value,
        w_query,
    )
    total_w, total_b = call(
        finish_kernel,
        "finish",
        2,
        (shape((9 * chans, 32), F32), shape((1, chans), F32)),
        [VMEM],
        (VMEM, VMEM),
        factor=1.0 / math.sqrt(4 * 96 * 512),
    )(summed.reshape(1024, LANES))
    near_back = exchange(near_grad)
    far_back = [lax.ppermute(far_grad[i], ALL, far_pairs(-i - 1)) for i in range(3)]
    base = call(
        back_kernel,
        "back",
        5,
        shape((tokens, chans), F32),
        [SMEM] + [VMEM] * 6,
        VMEM,
        [
            pltpu.VMEM(((rows + 2) * cols, 3 * chans), BF16),
            pltpu.VMEM((3 * chans, 3 * chans), BF16),
        ],
    )(where, slope, slope_top, slope_bottom, grad_flat, part, taps)
    grad_feats = call(
        join_kernel,
        "join",
        3,
        shape((tokens, chans), BF16),
        [SMEM, SMEM] + [VMEM] * 5,
        VMEM,
        [pltpu.VMEM((tokens, chans), F32)],
    )(where, table, base, near_back, *far_back)
    return (
        grad_feats.reshape(1, rows, cols, chans),
        total_w.reshape(conv_w.shape),
        total_b.reshape(chans),
    )


def solution(mesh):
    split = Mesh(mesh.devices.reshape(2, 2, 4, 4, 2), ALL)
    whole = P(("high", "core"), ("x", "z", "low"), None, None)
    return jax.shard_map(
        shards,
        mesh=split,
        in_specs=(whole, whole) + (P(),) * 10,
        out_specs=(whole, P(), P()),
        check_vma=False,
    )
```

```python
import functools
import math

import jax
import jax.numpy as jnp
from jax import lax
from jax.experimental import pallas as pl
from jax.experimental.pallas import tpu as pltpu
from jax.sharding import Mesh
from jax.sharding import PartitionSpec as P

F32 = jnp.float32
BF16 = jnp.bfloat16
BLK = 128
PAIR = 2 * BLK
HEAD_DIM = 64
LANES = 128
DEAD = -1e30
HALF = 296
VMEM = pl.BlockSpec(memory_space=pltpu.VMEM)
SMEM = pl.BlockSpec(memory_space=pltpu.SMEM)
BIG = pltpu.CompilerParams(vmem_limit_bytes=56 << 20)


def dot(a, b):
    return jnp.dot(a, b, preferred_element_type=F32)


def dot_t(a, b):
    return lax.dot_general(a, b, (((1,), (1,)), ((), ())), preferred_element_type=F32)


def entry(source_view, source_strip, view, offset):
    return ((source_view * 32 + source_strip) * 4 + view) * 3 + offset


def row_of(block):
    return block // 9 * HALF + block % 9 * 32


def offset_of(other, low):
    return 1 + other - low


def pack_kernel(place_ref, table_ref, flat_ref, near_ref, far0_ref, far1_ref, far2_ref):
    camera, strip = place_ref[0], place_ref[1]
    low = lax.rem(strip, 2)

    def blocks(view, offset):
        start = table_ref[3 * view + offset]
        return flat_ref[pl.ds(pl.multiple_of(start * BLK, BLK), PAIR), :]

    for view in range(4):
        for other in range(2):
            near_ref[2 * view + other] = blocks(view, offset_of(other, low))
    for shift, far_ref in enumerate((far0_ref, far1_ref, far2_ref)):
        far_ref[...] = blocks(lax.rem(camera + 1 + shift, 4), 2 * low)


def project_kernel(flat_ref, grad_ref, wq_ref, wo_ref, query_ref, out_ref):
    query = dot(flat_ref[...], wq_ref[...]).astype(BF16)
    query_ref[...] = query * BF16(1.0 / math.sqrt(HEAD_DIM))
    out_ref[...] = dot_t(grad_ref[...], wo_ref[...]).astype(BF16)


def spread(rows_ref, tap):
    block = rows_ref[tap * 256 : (tap + 1) * 256, :]
    width = block.shape[1]
    pick = lax.broadcasted_iota(jnp.int32, (width, 256), 1) % width
    same = pick == lax.broadcasted_iota(jnp.int32, (width, 256), 0)
    tiled = dot(block, same.astype(F32).astype(BF16))
    row = lax.broadcasted_iota(jnp.int32, (256, 256), 0) // width
    lane = lax.broadcasted_iota(jnp.int32, (256, 256), 1) // width
    return jnp.where(row == lane, tiled, 0.0).astype(BF16)


def shifted(row):
    cols = row.shape[0]
    wide = row.astype(F32)
    column = lax.broadcasted_iota(jnp.int32, wide.shape, 0)
    before = jnp.where(column == 0, 0.0, pltpu.roll(wide, 1, 0))
    after = jnp.where(column == cols - 1, 0.0, pltpu.roll(wide, cols - 1, 0))
    return before.astype(BF16), row, after.astype(BF16)


def fill_padded(place_ref, pad_ref, top_ref, flat_ref, bottom_ref, cols, rows):
    strip = place_ref[1]
    for r in range(rows + 2):
        if r == 0:
            line = jnp.where(strip > 0, top_ref[...], 0)
        elif r == rows + 1:
            line = jnp.where(strip < 31, bottom_ref[...], 0)
        else:
            line = flat_ref[(r - 1) * cols : r * cols, :]
        for dx, part in enumerate(shifted(line)):
            pad_ref[r * cols : (r + 1) * cols, dx * 256 : (dx + 1) * 256] = part


def conv_kernel(
    place_ref, flat_ref, top_ref, bottom_ref, grad_ref, w_ref, b_ref, slope_ref, first_ref, last_ref, sums_ref, pad_ref, wide_ref, turn_ref
):
    cols = top_ref.shape[0]
    rows = flat_ref.shape[0] // cols
    fill_padded(place_ref, pad_ref, top_ref, flat_ref, bottom_ref, cols, rows)
    for tap in range(9):
        wide_ref[tap * 256 : (tap + 1) * 256, :] = spread(w_ref, tap)
    bias_sum = jnp.zeros((1, 256), F32)
    for r in range(rows):
        act = b_ref[...]
        for dy in range(3):
            act = act + dot(
                pad_ref[(r + dy) * cols : (r + dy + 1) * cols, :], wide_ref[dy * 768 : (dy + 1) * 768, :]
            )
        square = act * act
        bent = jnp.tanh(0.7978845608028654 * (act + 0.044715 * square * act))
        inner = 0.7978845608028654 * (1.0 + 3.0 * 0.044715 * square)
        gain = 0.5 * (1.0 + bent) + 0.5 * act * (1.0 - bent * bent) * inner
        slope = grad_ref[r * cols : (r + 1) * cols, :].astype(F32) * gain
        bias_sum = bias_sum + jnp.sum(slope, axis=0, keepdims=True)
        slope_b = slope.astype(BF16)
        slope_ref[r * cols : (r + 1) * cols, :] = slope_b
        turn_ref[:, r * cols : (r + 1) * cols] = slope_b.T
        if r == 0:
            first_ref[...] = slope_b
        if r == rows - 1:
            last_ref[...] = slope_b
    lane_group = lax.broadcasted_iota(jnp.int32, (32, LANES), 1) // 32
    for dy in range(3):
        full = dot(turn_ref[...], pad_ref[dy * cols : (dy + rows) * cols, :])
        for dx in range(3):
            for half in range(2):
                part = full[half * LANES : (half + 1) * LANES, dx * 256 + half * LANES : dx * 256 + (half + 1) * LANES]
                packed = jnp.zeros((32, LANES), F32)
                for g in range(4):
                    packed = packed + jnp.where(lane_group == g, part[g * 32 : (g + 1) * 32, :], 0.0)
                at = row_of((3 * dy + dx) * 2 + half)
                sums_ref[at : at + 32, :] = packed
    sums_ref[2 * HALF :, :] = jnp.zeros((sums_ref.shape[0] - 2 * HALF, LANES), F32)
    for half in range(2):
        at = half * HALF + HALF - 8
        sums_ref[at : at + 8, :] = jnp.broadcast_to(bias_sum[:, half * LANES : (half + 1) * LANES], (8, LANES))


def back_kernel(place_ref, slope_ref, top_ref, bottom_ref, grad_ref, part_ref, w_ref, base_ref, pad_ref, wide_ref):
    cols = top_ref.shape[0]
    rows = slope_ref.shape[0] // cols
    fill_padded(place_ref, pad_ref, top_ref, slope_ref, bottom_ref, cols, rows)
    for tap in range(9):
        dy, dx = tap // 3, tap % 3
        wide_ref[dy * 256 : (dy + 1) * 256, (2 - dx) * 256 : (3 - dx) * 256] = spread(w_ref, tap)
    for r in range(rows):
        total = grad_ref[r * cols : (r + 1) * cols, :].astype(F32) + part_ref[r * cols : (r + 1) * cols, :]
        for dy in range(3):
            total = total + dot_t(
                pad_ref[(r + 2 - dy) * cols : (r + 3 - dy) * cols, :], wide_ref[dy * 256 : (dy + 1) * 256, :]
            )
        base_ref[r * cols : (r + 1) * cols, :] = total


def attend_kernel(
    place_ref,
    frame_ref,
    blocks_ref,
    near_ref,
    far0_ref,
    far1_ref,
    far2_ref,
    table_ref,
    query_ref,
    grad_ref,
    wk_ref,
    wv_ref,
    wq_ref,
    near_out_ref,
    far0_out_ref,
    far1_out_ref,
    far2_out_ref,
    part_ref,
    key_s,
    value_s,
    turn_s,
    key_grad_s,
    value_grad_s,
    score_s,
    pull_s,
    score_grad_s,
    probs_s,
    *,
    span,
):
    camera, strip = place_ref[0], place_ref[1]
    low = lax.rem(strip, 2)
    pair = strip - low
    far_strip = strip + 2 * low - 1
    inside = jnp.logical_and(far_strip >= 0, far_strip < 32)
    far_safe = jnp.clip(far_strip, 0, 31)
    tokens = query_ref.shape[0]
    groups = []
    for shift in range(3):
        view = lax.rem(camera + 1 + shift, 4)
        for other in range(2):
            count = blocks_ref[entry(view, pair + other, camera, offset_of(low, other))]
            groups.append((near_ref.at[2 * view + other], near_out_ref.at[2 * view + other], view, count))
    fars = ((far0_ref, far0_out_ref), (far1_ref, far1_out_ref), (far2_ref, far2_out_ref))
    for shift in range(3):
        view = lax.rem(camera + 3 - shift, 4)
        count = jnp.where(inside, blocks_ref[entry(view, far_safe, camera, 2 - 2 * low)], 0)
        groups.append(fars[shift] + (view, count))
    biases = []
    for i, (source, _, view, count) in enumerate(groups):
        rows = slice(i * PAIR, (i + 1) * PAIR)
        embed = table_ref[pl.ds(frame_ref[view], 1), :]
        entering = (source[...].astype(F32) + embed).astype(BF16)
        keys = dot(entering, wk_ref[...]).astype(BF16)
        key_s[rows, :] = keys
        value_s[rows, :] = dot(entering, wv_ref[...]).astype(BF16)
        turn_s[:, rows] = keys.T
        biases += [jnp.where(count > b, 0.0, DEAD).astype(F32) for b in range(2)]
    key_grad_s[...] = jnp.zeros_like(key_grad_s)
    value_grad_s[...] = jnp.zeros_like(value_grad_s)
    first_head = lax.broadcasted_iota(jnp.int32, (span, LANES), 1) < HEAD_DIM
    both = 2 * span

    def tile(t, carry):
        here = pl.ds(pl.multiple_of(t * span, span), span)
        found = []
        for p in range(2):
            lanes = slice(p * LANES, (p + 1) * LANES)
            query, grad = query_ref[here, lanes], grad_ref[here, lanes]
            zero = jnp.zeros_like(query)
            queries = jnp.concatenate(
                [jnp.where(first_head, query, zero), jnp.where(first_head, zero, query)], 0
            )
            grads = jnp.concatenate(
                [jnp.where(first_head, grad, zero), jnp.where(first_head, zero, grad)], 0
            )
            score_s[...] = dot_t(key_s[:, lanes], queries)
            pull_s[...] = dot_t(value_s[:, lanes], grads)
            chunks = [(slice(c * BLK, (c + 1) * BLK), bias) for c, bias in enumerate(biases)]
            highest = None
            for rows, bias in chunks:
                top = jnp.max(score_s[rows, :].reshape(BLK // 8, 8, both), 0) + bias
                highest = top if highest is None else jnp.maximum(highest, top)
            highest = jnp.max(highest, 0, keepdims=True)
            norm, delta = 0.0, 0.0
            for rows, bias in chunks:
                weight = jnp.exp(score_s[rows, :] - (highest - bias))
                norm = norm + jnp.sum(weight.reshape(BLK // 8, 8, both), 0)
                delta = delta + jnp.sum((weight * pull_s[rows, :]).reshape(BLK // 8, 8, both), 0)
            norm = jnp.sum(norm, 0, keepdims=True)
            delta = jnp.sum(delta, 0, keepdims=True) / norm
            level = highest + jnp.log(norm)
            for rows, bias in chunks:
                probs = jnp.exp(score_s[rows, :] - (level - bias))
                score_grad_s[rows, :] = (probs * (pull_s[rows, :] - delta)).astype(BF16)
                probs_s[rows, :] = probs.astype(BF16)
            key_grad_s[:, lanes] += dot(score_grad_s[...], queries)
            value_grad_s[:, lanes] += dot(probs_s[...], grads)
            head = p * LANES
            upper = dot(turn_s[head : head + HEAD_DIM, :], score_grad_s[:, :span])
            lower = dot(turn_s[head + HEAD_DIM : head + LANES, :], score_grad_s[:, span:])
            found += [upper, lower]
        query_grad = (jnp.concatenate(found, 0) * (1.0 / math.sqrt(HEAD_DIM))).T.astype(BF16)
        part_ref[here, :] = dot_t(query_grad, wq_ref[...])
        return carry

    lax.fori_loop(0, tokens // span, tile, 0)
    for i, (_, target, _, _) in enumerate(groups):
        rows = slice(i * PAIR, (i + 1) * PAIR)
        sent = dot_t(key_grad_s[rows, :].astype(BF16), wk_ref[...])
        sent = sent + dot_t(value_grad_s[rows, :].astype(BF16), wv_ref[...])
        target[...] = sent.astype(BF16)


def join_kernel(place_ref, table_ref, part_ref, near_ref, far0_ref, far1_ref, far2_ref, out_ref, total_s):
    camera, strip = place_ref[0], place_ref[1]
    low = lax.rem(strip, 2)
    total_s[...] = part_ref[...]

    def add(start, block):
        rows = pl.ds(pl.multiple_of(start * BLK, BLK), PAIR)
        total_s[rows, :] += block.astype(F32)

    for shift in range(3):
        view = lax.rem(camera + 1 + shift, 4)
        for other in range(2):
            add(table_ref[3 * view + offset_of(other, low)], near_ref[2 * view + other])
        add(table_ref[3 * view + 2 * low], (far0_ref, far1_ref, far2_ref)[shift][...])
    out_ref[...] = total_s[...].astype(BF16)


def sum_kernel(pieces_ref, out_ref):
    out_ref[...] = jnp.broadcast_to(jnp.sum(pieces_ref[...], 0, keepdims=True), out_ref.shape)


def finish_kernel(sums_ref, w_ref, b_ref, *, factor):
    for block in range(18):
        at = row_of(block)
        w_ref[block * LANES : (block + 1) * LANES, :] = (sums_ref[at : at + 32, :] * factor).T
    b_ref[:, :LANES] = sums_ref[HALF - 8 : HALF - 7, :] * factor
    b_ref[:, LANES:] = sums_ref[2 * HALF - 8 : 2 * HALF - 7, :] * factor


def call(kernel, name, micros, out, ins, outs, scratch=(), **options):
    cost = pl.CostEstimate(flops=int(micros * 1e9), bytes_accessed=int(micros * 3e6), transcendentals=0)
    return pl.pallas_call(
        functools.partial(kernel, **options),
        out_shape=out,
        in_specs=ins,
        out_specs=outs,
        scratch_shapes=list(scratch),
        compiler_params=BIG,
        cost_estimate=cost,
        name=name,
    )


def shape(dims, kind):
    return jax.ShapeDtypeStruct(dims, kind)


ALL = ("high", "core", "x", "z", "low")
RING = ("high", "core", "low")


def place(camera, strip):
    return camera * 32 + strip


def neighbours(step):
    return [(place(c, s), place(c, (s + step) % 32)) for c in range(4) for s in range(32)]


def far_pairs(shift):
    return [
        (place(c, s), place((c + shift) % 4, (s + 1 if s % 2 else s - 1) % 32))
        for c in range(4)
        for s in range(32)
    ]


def exchange(block):
    return lax.all_to_all(block, RING, split_axis=0, concat_axis=0, tiled=True)


def shards(
    feats,
    cotangent,
    conv_w,
    conv_b,
    w_query,
    w_key,
    w_value,
    w_out,
    time_table,
    frame_index,
    block_start,
    block_count,
):
    rows, cols, chans = feats.shape[1:]
    tokens = rows * cols
    keys = 9 * PAIR
    core = lax.axis_index("core")
    camera = 2 * lax.axis_index("high") + core
    strip = 8 * lax.axis_index("x") + 2 * lax.axis_index("z") + lax.axis_index("low")
    where = jnp.stack([camera, strip]).astype(jnp.int32)
    flat = feats.reshape(tokens, chans)
    grad_flat = cotangent.reshape(tokens, chans)
    starts = lax.dynamic_slice(block_start, (camera, strip, 0, 0), (1, 1, 4, 3)).reshape(12)
    taps = conv_w.reshape(-1, conv_w.shape[-1])

    row = shape((cols, chans), BF16)
    slot = shape((PAIR, chans), BF16)
    slots = shape((8, PAIR, chans), BF16)
    top = lax.ppermute(flat[tokens - cols :], ALL, neighbours(1))
    bottom = lax.ppermute(flat[:cols], ALL, neighbours(-1))
    near, *far = call(
        pack_kernel,
        "pack",
        3,
        (slots, slot, slot, slot),
        [SMEM, SMEM, VMEM],
        (VMEM,) * 4,
    )(where, starts, flat)
    flat_conv, near, block_count = lax.optimization_barrier((flat, near, block_count))
    counts = block_count.reshape(-1)
    near = exchange(near)
    far = [lax.ppermute(far[i], ALL, far_pairs(i + 1)) for i in range(3)]
    slope, slope_first, slope_last, sums = call(
        conv_kernel,
        "conv",
        8,
        (shape((tokens, chans), BF16), row, row, shape((1024, LANES), F32)),
        [SMEM] + [VMEM] * 6,
        (VMEM,) * 4,
        [
            pltpu.VMEM(((rows + 2) * cols, 3 * chans), BF16),
            pltpu.VMEM((9 * chans, chans), BF16),
            pltpu.VMEM((chans, tokens), BF16),
        ],
    )(where, flat_conv, top, bottom, grad_flat, taps, conv_b.reshape(1, chans))

    near, *far, sums, flat_next = lax.optimization_barrier((near, *far, sums, flat))
    pieces = lax.all_to_all(sums.reshape(128, 8, LANES), ALL, split_axis=0, concat_axis=0, tiled=True)
    query, out_grad = call(
        project_kernel,
        "project",
        3,
        (shape((tokens, chans), BF16), shape((tokens, chans), BF16)),
        [VMEM] * 4,
        (VMEM,) * 2,
    )(flat_next, grad_flat, w_query, w_out)
    pieces = call(sum_kernel, "add_pieces", 2, shape((128, 8, LANES), F32), [VMEM], VMEM)(pieces)
    pieces, near, query, slope_first, slope_last = lax.optimization_barrier(
        (pieces, near, query, slope_first, slope_last)
    )
    slope_top = lax.ppermute(slope_last, ALL, neighbours(1))
    slope_bottom = lax.ppermute(slope_first, ALL, neighbours(-1))
    summed = lax.all_to_all(pieces, ALL, split_axis=0, concat_axis=0, tiled=True)

    span = 512
    near_grad, *far_grad, part = call(
        attend_kernel,
        "attend",
        58,
        (
            slots,
            slot,
            slot,
            slot,
            shape((tokens, chans), F32),
        ),
        [SMEM, SMEM, SMEM] + [VMEM] * 10,
        (VMEM,) * 5,
        [
            pltpu.VMEM((keys, chans), BF16),
            pltpu.VMEM((keys, chans), BF16),
            pltpu.VMEM((chans, keys), BF16),
            pltpu.VMEM((keys, chans), F32),
            pltpu.VMEM((keys, chans), F32),
            pltpu.VMEM((keys, 2 * span), F32),
            pltpu.VMEM((keys, 2 * span), F32),
            pltpu.VMEM((keys, 2 * span), BF16),
            pltpu.VMEM((keys, 2 * span), BF16),
        ],
        span=span,
    )(
        where,
        frame_index,
        counts,
        near,
        *far,
        time_table.astype(F32),
        query,
        out_grad,
        w_key,
        w_value,
        w_query,
    )
    total_w, total_b = call(
        finish_kernel,
        "finish",
        2,
        (shape((9 * chans, 32), F32), shape((1, chans), F32)),
        [VMEM],
        (VMEM, VMEM),
        factor=1.0 / math.sqrt(4 * 96 * 512),
    )(summed.reshape(1024, LANES))
    near_back = exchange(near_grad)
    far_back = [lax.ppermute(far_grad[i], ALL, far_pairs(-i - 1)) for i in range(3)]
    base = call(
        back_kernel,
        "back",
        5,
        shape((tokens, chans), F32),
        [SMEM] + [VMEM] * 6,
        VMEM,
        [
            pltpu.VMEM(((rows + 2) * cols, 3 * chans), BF16),
            pltpu.VMEM((3 * chans, 3 * chans), BF16),
        ],
    )(where, slope, slope_top, slope_bottom, grad_flat, part, taps)
    grad_feats = call(
        join_kernel,
        "join",
        3,
        shape((tokens, chans), BF16),
        [SMEM, SMEM] + [VMEM] * 5,
        VMEM,
        [pltpu.VMEM((tokens, chans), F32)],
    )(where, starts, base, near_back, *far_back)
    return (
        grad_feats.reshape(1, rows, cols, chans),
        total_w.reshape(conv_w.shape),
        total_b.reshape(chans),
    )


def solution(mesh):
    split = Mesh(mesh.devices.reshape(2, 2, 4, 4, 2), ALL)
    whole = P(("high", "core"), ("x", "z", "low"), None, None)
    return jax.shard_map(
        shards,
        mesh=split,
        in_specs=(whole, whole) + (P(),) * 10,
        out_specs=(whole, P(), P()),
        check_vma=False,
    )
```

```python
import functools
import math

import jax
import jax.numpy as jnp
from jax import lax
from jax.experimental import pallas as pl
from jax.experimental.pallas import tpu as pltpu
from jax.sharding import Mesh
from jax.sharding import PartitionSpec as P

F32 = jnp.float32
BF16 = jnp.bfloat16
BLK = 128
PAIR = 2 * BLK
HEAD_DIM = 64
LANES = 128
DEAD = -1e30
HALF = 296
VMEM = pl.BlockSpec(memory_space=pltpu.VMEM)
SMEM = pl.BlockSpec(memory_space=pltpu.SMEM)
BIG = pltpu.CompilerParams(vmem_limit_bytes=56 << 20)


def dot(a, b):
    return jnp.dot(a, b, preferred_element_type=F32)


def dot_t(a, b):
    return lax.dot_general(a, b, (((1,), (1,)), ((), ())), preferred_element_type=F32)


def entry(source_view, source_strip, view, offset):
    return ((source_view * 32 + source_strip) * 4 + view) * 3 + offset


def row_of(block):
    return block // 9 * HALF + block % 9 * 32


def offset_of(other, low):
    return 1 + other - low


def pack_kernel(place_ref, table_ref, flat_ref, near_ref, far0_ref, far1_ref, far2_ref):
    camera, strip = place_ref[0], place_ref[1]
    low = lax.rem(strip, 2)

    def blocks(view, offset):
        start = table_ref[3 * view + offset]
        return flat_ref[pl.ds(pl.multiple_of(start * BLK, BLK), PAIR), :]

    for view in range(4):
        for other in range(2):
            near_ref[2 * view + other] = blocks(view, offset_of(other, low))
    for shift, far_ref in enumerate((far0_ref, far1_ref, far2_ref)):
        far_ref[...] = blocks(lax.rem(camera + 1 + shift, 4), 2 * low)


def project_kernel(flat_ref, grad_ref, wq_ref, wo_ref, query_ref, out_ref):
    query = dot(flat_ref[...], wq_ref[...]).astype(BF16)
    query_ref[...] = query * BF16(1.0 / math.sqrt(HEAD_DIM))
    out_ref[...] = dot_t(grad_ref[...], wo_ref[...]).astype(BF16)


def spread(rows_ref, tap):
    block = rows_ref[tap * 256 : (tap + 1) * 256, :]
    width = block.shape[1]
    pick = lax.broadcasted_iota(jnp.int32, (width, 256), 1) % width
    same = pick == lax.broadcasted_iota(jnp.int32, (width, 256), 0)
    tiled = dot(block, same.astype(F32).astype(BF16))
    row = lax.broadcasted_iota(jnp.int32, (256, 256), 0) // width
    lane = lax.broadcasted_iota(jnp.int32, (256, 256), 1) // width
    return jnp.where(row == lane, tiled, 0.0).astype(BF16)


def shifted(row):
    cols = row.shape[0]
    wide = row.astype(F32)
    column = lax.broadcasted_iota(jnp.int32, wide.shape, 0)
    before = jnp.where(column == 0, 0.0, pltpu.roll(wide, 1, 0))
    after = jnp.where(column == cols - 1, 0.0, pltpu.roll(wide, cols - 1, 0))
    return before.astype(BF16), row, after.astype(BF16)


def fill_padded(place_ref, pad_ref, top_ref, flat_ref, bottom_ref, cols, rows):
    strip = place_ref[1]
    for r in range(rows + 2):
        if r == 0:
            line = jnp.where(strip > 0, top_ref[...], 0)
        elif r == rows + 1:
            line = jnp.where(strip < 31, bottom_ref[...], 0)
        else:
            line = flat_ref[(r - 1) * cols : r * cols, :]
        for dx, part in enumerate(shifted(line)):
            pad_ref[r * cols : (r + 1) * cols, dx * 256 : (dx + 1) * 256] = part


def conv_kernel(
    place_ref, flat_ref, top_ref, bottom_ref, grad_ref, w_ref, b_ref, slope_ref, first_ref, last_ref, sums_ref, pad_ref, wide_ref, turn_ref
):
    cols = top_ref.shape[0]
    rows = flat_ref.shape[0] // cols
    fill_padded(place_ref, pad_ref, top_ref, flat_ref, bottom_ref, cols, rows)
    for tap in range(9):
        wide_ref[tap * 256 : (tap + 1) * 256, :] = spread(w_ref, tap)
    bias_sum = jnp.zeros((1, 256), F32)
    for r in range(rows):
        act = b_ref[...]
        for dy in range(3):
            act = act + dot(
                pad_ref[(r + dy) * cols : (r + dy + 1) * cols, :], wide_ref[dy * 768 : (dy + 1) * 768, :]
            )
        square = act * act
        bent = jnp.tanh(0.7978845608028654 * (act + 0.044715 * square * act))
        inner = 0.7978845608028654 * (1.0 + 3.0 * 0.044715 * square)
        gain = 0.5 * (1.0 + bent) + 0.5 * act * (1.0 - bent * bent) * inner
        slope = grad_ref[r * cols : (r + 1) * cols, :].astype(F32) * gain
        bias_sum = bias_sum + jnp.sum(slope, axis=0, keepdims=True)
        slope_b = slope.astype(BF16)
        slope_ref[r * cols : (r + 1) * cols, :] = slope_b
        turn_ref[:, r * cols : (r + 1) * cols] = slope_b.T
        if r == 0:
            first_ref[...] = slope_b
        if r == rows - 1:
            last_ref[...] = slope_b
    lane_group = lax.broadcasted_iota(jnp.int32, (32, LANES), 1) // 32
    for dy in range(3):
        full = dot(turn_ref[...], pad_ref[dy * cols : (dy + rows) * cols, :])
        for dx in range(3):
            for half in range(2):
                part = full[half * LANES : (half + 1) * LANES, dx * 256 + half * LANES : dx * 256 + (half + 1) * LANES]
                packed = jnp.zeros((32, LANES), F32)
                for g in range(4):
                    packed = packed + jnp.where(lane_group == g, part[g * 32 : (g + 1) * 32, :], 0.0)
                at = row_of((3 * dy + dx) * 2 + half)
                sums_ref[at : at + 32, :] = packed
    sums_ref[2 * HALF :, :] = jnp.zeros((sums_ref.shape[0] - 2 * HALF, LANES), F32)
    for half in range(2):
        at = half * HALF + HALF - 8
        sums_ref[at : at + 8, :] = jnp.broadcast_to(bias_sum[:, half * LANES : (half + 1) * LANES], (8, LANES))


def back_kernel(place_ref, slope_ref, top_ref, bottom_ref, grad_ref, part_ref, w_ref, base_ref, pad_ref, wide_ref):
    cols = top_ref.shape[0]
    rows = slope_ref.shape[0] // cols
    fill_padded(place_ref, pad_ref, top_ref, slope_ref, bottom_ref, cols, rows)
    for tap in range(9):
        dy, dx = tap // 3, tap % 3
        wide_ref[dy * 256 : (dy + 1) * 256, (2 - dx) * 256 : (3 - dx) * 256] = spread(w_ref, tap)
    for r in range(rows):
        total = grad_ref[r * cols : (r + 1) * cols, :].astype(F32) + part_ref[r * cols : (r + 1) * cols, :]
        for dy in range(3):
            total = total + dot_t(
                pad_ref[(r + 2 - dy) * cols : (r + 3 - dy) * cols, :], wide_ref[dy * 256 : (dy + 1) * 256, :]
            )
        base_ref[r * cols : (r + 1) * cols, :] = total


def attend_kernel(
    place_ref,
    frame_ref,
    blocks_ref,
    near_ref,
    far0_ref,
    far1_ref,
    far2_ref,
    table_ref,
    query_ref,
    grad_ref,
    wk_ref,
    wv_ref,
    wq_ref,
    near_out_ref,
    far0_out_ref,
    far1_out_ref,
    far2_out_ref,
    part_ref,
    key_s,
    value_s,
    turn_s,
    key_grad_s,
    value_grad_s,
    score_s,
    pull_s,
    score_grad_s,
    probs_s,
    *,
    span,
):
    camera, strip = place_ref[0], place_ref[1]
    low = lax.rem(strip, 2)
    pair = strip - low
    far_strip = strip + 2 * low - 1
    inside = jnp.logical_and(far_strip >= 0, far_strip < 32)
    far_safe = jnp.clip(far_strip, 0, 31)
    tokens = query_ref.shape[0]
    groups = []
    for shift in range(3):
        view = lax.rem(camera + 1 + shift, 4)
        for other in range(2):
            count = blocks_ref[entry(view, pair + other, camera, offset_of(low, other))]
            groups.append((near_ref.at[2 * view + other], near_out_ref.at[2 * view + other], view, count))
    fars = ((far0_ref, far0_out_ref), (far1_ref, far1_out_ref), (far2_ref, far2_out_ref))
    for shift in range(3):
        view = lax.rem(camera + 3 - shift, 4)
        count = jnp.where(inside, blocks_ref[entry(view, far_safe, camera, 2 - 2 * low)], 0)
        groups.append(fars[shift] + (view, count))
    biases = []
    for i, (source, _, view, count) in enumerate(groups):
        rows = slice(i * PAIR, (i + 1) * PAIR)
        embed = table_ref[pl.ds(frame_ref[view], 1), :]
        entering = (source[...].astype(F32) + embed).astype(BF16)
        keys = dot(entering, wk_ref[...]).astype(BF16)
        key_s[rows, :] = keys
        value_s[rows, :] = dot(entering, wv_ref[...]).astype(BF16)
        turn_s[:, rows] = keys.T
        biases += [jnp.where(count > b, 0.0, DEAD).astype(F32) for b in range(2)]
    key_grad_s[...] = jnp.zeros_like(key_grad_s)
    value_grad_s[...] = jnp.zeros_like(value_grad_s)
    first_head = lax.broadcasted_iota(jnp.int32, (span, LANES), 1) < HEAD_DIM
    both = 2 * span

    def tile(t, carry):
        here = pl.ds(pl.multiple_of(t * span, span), span)
        found = []
        for p in range(2):
            lanes = slice(p * LANES, (p + 1) * LANES)
            query, grad = query_ref[here, lanes], grad_ref[here, lanes]
            zero = jnp.zeros_like(query)
            queries = jnp.concatenate(
                [jnp.where(first_head, query, zero), jnp.where(first_head, zero, query)], 0
            )
            grads = jnp.concatenate(
                [jnp.where(first_head, grad, zero), jnp.where(first_head, zero, grad)], 0
            )
            score_s[...] = dot_t(key_s[:, lanes], queries)
            pull_s[...] = dot_t(value_s[:, lanes], grads)
            chunks = [(slice(c * BLK, (c + 1) * BLK), bias) for c, bias in enumerate(biases)]
            highest = None
            for rows, bias in chunks:
                top = jnp.max(score_s[rows, :].reshape(BLK // 8, 8, both), 0) + bias
                highest = top if highest is None else jnp.maximum(highest, top)
            highest = jnp.max(highest, 0, keepdims=True)
            norm, delta = 0.0, 0.0
            for rows, bias in chunks:
                weight = jnp.exp(score_s[rows, :] - (highest - bias))
                norm = norm + jnp.sum(weight.reshape(BLK // 8, 8, both), 0)
                delta = delta + jnp.sum((weight * pull_s[rows, :]).reshape(BLK // 8, 8, both), 0)
            norm = jnp.sum(norm, 0, keepdims=True)
            delta = jnp.sum(delta, 0, keepdims=True) / norm
            level = highest + jnp.log(norm)
            for rows, bias in chunks:
                probs = jnp.exp(score_s[rows, :] - (level - bias))
                score_grad_s[rows, :] = (probs * (pull_s[rows, :] - delta)).astype(BF16)
                probs_s[rows, :] = probs.astype(BF16)
            key_grad_s[:, lanes] += dot(score_grad_s[...], queries)
            value_grad_s[:, lanes] += dot(probs_s[...], grads)
            head = p * LANES
            upper = dot(turn_s[head : head + HEAD_DIM, :], score_grad_s[:, :span])
            lower = dot(turn_s[head + HEAD_DIM : head + LANES, :], score_grad_s[:, span:])
            found += [upper, lower]
        query_grad = (jnp.concatenate(found, 0) * (1.0 / math.sqrt(HEAD_DIM))).T.astype(BF16)
        part_ref[here, :] = dot_t(query_grad, wq_ref[...])
        return carry

    lax.fori_loop(0, tokens // span, tile, 0)
    for i, (_, target, _, _) in enumerate(groups):
        rows = slice(i * PAIR, (i + 1) * PAIR)
        sent = dot_t(key_grad_s[rows, :].astype(BF16), wk_ref[...])
        sent = sent + dot_t(value_grad_s[rows, :].astype(BF16), wv_ref[...])
        target[...] = sent.astype(BF16)


def join_kernel(place_ref, table_ref, part_ref, near_ref, far0_ref, far1_ref, far2_ref, out_ref, total_s):
    camera, strip = place_ref[0], place_ref[1]
    low = lax.rem(strip, 2)
    total_s[...] = part_ref[...]

    def add(start, block):
        rows = pl.ds(pl.multiple_of(start * BLK, BLK), PAIR)
        total_s[rows, :] += block.astype(F32)

    for shift in range(3):
        view = lax.rem(camera + 1 + shift, 4)
        for other in range(2):
            add(table_ref[3 * view + offset_of(other, low)], near_ref[2 * view + other])
        add(table_ref[3 * view + 2 * low], (far0_ref, far1_ref, far2_ref)[shift][...])
    out_ref[...] = total_s[...].astype(BF16)


def sum_kernel(pieces_ref, out_ref):
    out_ref[...] = jnp.broadcast_to(jnp.sum(pieces_ref[...], 0, keepdims=True), out_ref.shape)


def finish_kernel(sums_ref, w_ref, b_ref, *, factor):
    for block in range(18):
        at = row_of(block)
        w_ref[block * LANES : (block + 1) * LANES, :] = (sums_ref[at : at + 32, :] * factor).T
    b_ref[:, :LANES] = sums_ref[HALF - 8 : HALF - 7, :] * factor
    b_ref[:, LANES:] = sums_ref[2 * HALF - 8 : 2 * HALF - 7, :] * factor


def call(kernel, name, micros, out, ins, outs, scratch=(), **options):
    cost = pl.CostEstimate(flops=int(micros * 1e9), bytes_accessed=int(micros * 3e6), transcendentals=0)
    return pl.pallas_call(
        functools.partial(kernel, **options),
        out_shape=out,
        in_specs=ins,
        out_specs=outs,
        scratch_shapes=list(scratch),
        compiler_params=BIG,
        cost_estimate=cost,
        name=name,
    )


def shape(dims, kind):
    return jax.ShapeDtypeStruct(dims, kind)


ALL = ("high", "core", "x", "z", "low")
RING = ("high", "core", "low")


def place(camera, strip):
    return camera * 32 + strip


def neighbours(step):
    return [(place(c, s), place(c, (s + step) % 32)) for c in range(4) for s in range(32)]


def far_pairs(shift):
    return [
        (place(c, s), place((c + shift) % 4, (s + 1 if s % 2 else s - 1) % 32))
        for c in range(4)
        for s in range(32)
    ]


def exchange(block):
    return lax.all_to_all(block, RING, split_axis=0, concat_axis=0, tiled=True)


def shards(
    feats,
    cotangent,
    conv_w,
    conv_b,
    w_query,
    w_key,
    w_value,
    w_out,
    time_table,
    frame_index,
    block_start,
    block_count,
):
    rows, cols, chans = feats.shape[1:]
    tokens = rows * cols
    keys = 9 * PAIR
    core = lax.axis_index("core")
    camera = 2 * lax.axis_index("high") + core
    strip = 8 * lax.axis_index("x") + 2 * lax.axis_index("z") + lax.axis_index("low")
    where = jnp.stack([camera, strip]).astype(jnp.int32)
    flat = feats.reshape(tokens, chans)
    grad_flat = cotangent.reshape(tokens, chans)
    starts = lax.dynamic_slice(block_start, (camera, strip, 0, 0), (1, 1, 4, 3)).reshape(12)
    taps = conv_w.reshape(-1, conv_w.shape[-1])

    row = shape((cols, chans), BF16)
    slot = shape((PAIR, chans), BF16)
    slots = shape((8, PAIR, chans), BF16)
    top = lax.ppermute(flat[tokens - cols :], ALL, neighbours(1))
    bottom = lax.ppermute(flat[:cols], ALL, neighbours(-1))
    near, *far = call(
        pack_kernel,
        "pack",
        3,
        (slots, slot, slot, slot),
        [SMEM, SMEM, VMEM],
        (VMEM,) * 4,
    )(where, starts, flat)
    flat_conv, near, block_count = lax.optimization_barrier((flat, near, block_count))
    counts = block_count.reshape(-1)
    near = exchange(near)
    far = [lax.ppermute(far[i], ALL, far_pairs(i + 1)) for i in range(3)]
    slope, slope_first, slope_last, sums = call(
        conv_kernel,
        "conv",
        8,
        (shape((tokens, chans), BF16), row, row, shape((1024, LANES), F32)),
        [SMEM] + [VMEM] * 6,
        (VMEM,) * 4,
        [
            pltpu.VMEM(((rows + 2) * cols, 3 * chans), BF16),
            pltpu.VMEM((9 * chans, chans), BF16),
            pltpu.VMEM((chans, tokens), BF16),
        ],
    )(where, flat_conv, top, bottom, grad_flat, taps, conv_b.reshape(1, chans))

    near, *far, sums, flat_next, slope_first, slope_last = lax.optimization_barrier(
        (near, *far, sums, flat, slope_first, slope_last)
    )
    pieces = lax.all_to_all(sums.reshape(128, 8, LANES), ALL, split_axis=0, concat_axis=0, tiled=True)
    slope_top = lax.ppermute(slope_last, ALL, neighbours(1))
    slope_bottom = lax.ppermute(slope_first, ALL, neighbours(-1))
    query, out_grad = call(
        project_kernel,
        "project",
        3,
        (shape((tokens, chans), BF16), shape((tokens, chans), BF16)),
        [VMEM] * 4,
        (VMEM,) * 2,
    )(flat_next, grad_flat, w_query, w_out)
    pieces = call(sum_kernel, "add_pieces", 2, shape((128, 8, LANES), F32), [VMEM], VMEM)(pieces)
    pieces, near, query = lax.optimization_barrier((pieces, near, query))
    summed = lax.all_to_all(pieces, ALL, split_axis=0, concat_axis=0, tiled=True)

    span = 512
    near_grad, *far_grad, part = call(
        attend_kernel,
        "attend",
        58,
        (
            slots,
            slot,
            slot,
            slot,
            shape((tokens, chans), F32),
        ),
        [SMEM, SMEM, SMEM] + [VMEM] * 10,
        (VMEM,) * 5,
        [
            pltpu.VMEM((keys, chans), BF16),
            pltpu.VMEM((keys, chans), BF16),
            pltpu.VMEM((chans, keys), BF16),
            pltpu.VMEM((keys, chans), F32),
            pltpu.VMEM((keys, chans), F32),
            pltpu.VMEM((keys, 2 * span), F32),
            pltpu.VMEM((keys, 2 * span), F32),
            pltpu.VMEM((keys, 2 * span), BF16),
            pltpu.VMEM((keys, 2 * span), BF16),
        ],
        span=span,
    )(
        where,
        frame_index,
        counts,
        near,
        *far,
        time_table.astype(F32),
        query,
        out_grad,
        w_key,
        w_value,
        w_query,
    )
    total_w, total_b = call(
        finish_kernel,
        "finish",
        2,
        (shape((9 * chans, 32), F32), shape((1, chans), F32)),
        [VMEM],
        (VMEM, VMEM),
        factor=1.0 / math.sqrt(4 * 96 * 512),
    )(summed.reshape(1024, LANES))
    near_back = exchange(near_grad)
    far_back = [lax.ppermute(far_grad[i], ALL, far_pairs(-i - 1)) for i in range(3)]
    base = call(
        back_kernel,
        "back",
        5,
        shape((tokens, chans), F32),
        [SMEM] + [VMEM] * 6,
        VMEM,
        [
            pltpu.VMEM(((rows + 2) * cols, 3 * chans), BF16),
            pltpu.VMEM((3 * chans, 3 * chans), BF16),
        ],
    )(where, slope, slope_top, slope_bottom, grad_flat, part, taps)
    grad_feats = call(
        join_kernel,
        "join",
        3,
        shape((tokens, chans), BF16),
        [SMEM, SMEM] + [VMEM] * 5,
        VMEM,
        [pltpu.VMEM((tokens, chans), F32)],
    )(where, starts, base, near_back, *far_back)
    return (
        grad_feats.reshape(1, rows, cols, chans),
        total_w.reshape(conv_w.shape),
        total_b.reshape(chans),
    )


def solution(mesh):
    split = Mesh(mesh.devices.reshape(2, 2, 4, 4, 2), ALL)
    whole = P(("high", "core"), ("x", "z", "low"), None, None)
    return jax.shard_map(
        shards,
        mesh=split,
        in_specs=(whole, whole) + (P(),) * 10,
        out_specs=(whole, P(), P()),
        check_vma=False,
    )
```
